32 devices in a mesh: groups: 2 (over y), seq: 4 (over z), blk: 2 (over x), hd: 2 (over core).
Axes of the slice: x: 2, y: 2, z: 4, core: 2. Of those that a mesh axis runs over, the one named last changes fastest.
Arguments:
- query_raw: bfloat16 [8192, 2048], P(('groups', 'seq', 'blk'), 'hd'), parts along dimension 0, may hold values from -6 to 6
- key_raw: bfloat16 [8192, 2048], P(('groups', 'seq', 'blk'), 'hd'), parts along dimension 0, may hold values from -6 to 6
- value_raw: bfloat16 [8192, 2048], P(('groups', 'seq', 'blk'), 'hd'), parts along dimension 0, may hold values from -6 to 6
- beta_rate: float32 [8192, 16], P(('groups', 'seq', 'blk'), 'hd'), parts along dimension 0, may hold values from 0 to 1
- conv_weight: float32 [3, 4, 2048], P(None, None, 'hd'), may hold values from -3 to 3
- out_gain: float32 [128], replicated, may hold values from 0.1 to 1.9
Outputs:
- head_output: bfloat16 [8192, 2048], P(('groups', 'seq', 'blk'), 'hd'), parts along dimension 0
The draws below stay inside these ranges and needn't reach their ends.
There are 2 independent parts, one for each index of `groups`. The reference program is written for one: setup_inputs(seed, part) draws one part's arguments, and reference() takes and returns one part's arrays. A program takes and returns all parts, laid end to end along the dimension named above; an argument that names none is the same for every part. Nothing has to cross between parts.
All inputs are finite; a program needn't handle non-finite values.
Results may differ from the reference program's by a relative error of at most 0.0064.
Values may be sent and summed in bfloat16 or wider, within the bound.
A program may use at most 192 MiB of HBM per device.

```python
import math
import jax
import jax.numpy as jnp
from jax import lax

HEADS = 16
KEY_SIZE = 128
DV = 128
CONV = 4
SPAN = 64
TOKEN_TOTAL = 4096


def draw_beta_rate(key, part):
    random_subkeys = jax.random.split(key, 6)
    token_positions = jnp.arange(TOKEN_TOTAL)
    fast_share = 0.5
    fast_heads = jax.random.uniform(random_subkeys[0], (HEADS,)) < fast_share
    fast_rate = jnp.exp(jax.random.uniform(random_subkeys[1], (HEADS,), minval=math.log(0.3), maxval=math.log(0.9)))
    slow_rate = jnp.exp(jax.random.uniform(random_subkeys[2], (HEADS,), minval=math.log(0.01), maxval=math.log(0.1)))
    base_rate = jnp.where(fast_heads, fast_rate, slow_rate)
    roughness = jnp.exp(jax.random.uniform(random_subkeys[3], (TOKEN_TOTAL, HEADS), minval=-math.log(2.0), maxval=math.log(2.0)))
    segment_count = TOKEN_TOTAL // 128 + 1
    segment_factor = jnp.exp(jax.random.uniform(random_subkeys[4], (segment_count, HEADS), minval=-math.log(2.0), maxval=math.log(2.0)))
    spread = segment_factor[token_positions // 128]
    segment_length = max(KEY_SIZE * 3 // 8, 1)
    segment_starts = jax.random.randint(random_subkeys[5], (3,), 0, TOKEN_TOTAL - segment_length)
    within_segment = jnp.any((token_positions[:, None] >= segment_starts[None, :]) & (token_positions[:, None] < segment_starts[None, :] + segment_length), axis=1)
    strength = jnp.minimum(base_rate[None, :] * roughness * spread, 1.0)
    return jnp.where(within_segment[:, None], 0.9, strength).astype(jnp.float32)


def shard_levels(rng, dims, cuts, least, largest):
    factor_of = 1.0
    for dim, shards_of in cuts:
        heights = jax.random.uniform(jax.random.fold_in(jax.random.fold_in(rng, 6), dim), (shards_of,), jnp.float32, least / len(cuts), largest / len(cuts))
        factor_of = factor_of * jnp.repeat(jnp.exp(heights), dims[dim] // shards_of).reshape((-1,) + (1,) * (len(dims) - 1 - dim))
    return factor_of


def bell_draw(stream_key, shape, scale, most, pieces=(), kind=jnp.bfloat16):
    entries = scale * jax.random.normal(stream_key, shape, jnp.float32)
    if pieces:
        entries = entries * shard_levels(stream_key, shape, pieces, -0.22, 0.18)
    return jnp.clip(entries, -most, most).astype(kind)


def setup_inputs(seed: int = 0, part: int = 0) -> dict:
    streams_of = jax.random.split(jax.random.key(seed), 7)
    part_keys = jax.random.split(jax.random.fold_in(streams_of[6], part), 7)
    query_raw = bell_draw(part_keys[0], (TOKEN_TOTAL, HEADS * KEY_SIZE), 1.0, 6.0, ((0, 8), (1, 2)))
    key_raw = bell_draw(part_keys[1], (TOKEN_TOTAL, HEADS * KEY_SIZE), 1.0, 6.0, ((0, 8), (1, 2)))
    value_raw = bell_draw(part_keys[2], (TOKEN_TOTAL, HEADS * DV), 1.0, 6.0, ((0, 8), (1, 2)))
    beta_rate = draw_beta_rate(jax.random.fold_in(jax.random.fold_in(streams_of[6], part), 71), part)
    conv_weight = bell_draw(streams_of[4], (3, CONV, HEADS * KEY_SIZE), CONV ** -0.5, 3.0, ((2, 2),), jnp.float32)
    out_gain = jnp.clip(1.0 + 0.18 * jax.random.normal(streams_of[5], (DV,), jnp.float32), 0.1, 1.9)
    return {"query_raw": query_raw, "key_raw": key_raw, "value_raw": value_raw, "beta_rate": beta_rate, "conv_weight": conv_weight, "out_gain": out_gain}


PRECISE = lax.Precision.HIGHEST

def short_conv(raw, weights):
    kernel_len = weights.shape[0]
    tok_rows = raw.shape[0]
    padded = jnp.pad(raw.astype(jnp.float32), ((kernel_len - 1, 0), (0, 0)))
    summed = jnp.zeros(raw.shape, jnp.float32)
    for offset in range(kernel_len):
        summed = summed + weights[offset] * padded[offset:offset + tok_rows]
    return jax.nn.silu(summed)

def reference(query_raw, key_raw, value_raw, beta_rate, conv_weight, out_gain):
    queries = short_conv(query_raw, conv_weight[0]).astype(jnp.bfloat16)
    conv_k = short_conv(key_raw, conv_weight[1]).reshape(TOKEN_TOTAL, HEADS, KEY_SIZE)
    keys_norm = (conv_k * lax.rsqrt(lax.optimization_barrier(jnp.sum(conv_k * conv_k, axis=-1, keepdims=True)) + 1e-06)).astype(jnp.bfloat16)
    values = short_conv(value_raw, conv_weight[2]).astype(jnp.bfloat16)
    span_count = TOKEN_TOTAL // SPAN
    q_blocks = jnp.transpose(queries.reshape(span_count, SPAN, HEADS, KEY_SIZE), (0, 2, 1, 3))
    k_blocks = jnp.transpose(keys_norm.reshape(span_count, SPAN, HEADS, KEY_SIZE), (0, 2, 1, 3))
    v_blocks = jnp.transpose(values.reshape(span_count, SPAN, HEADS, DV), (0, 2, 1, 3))
    rate_blocks = jnp.transpose(beta_rate.reshape(span_count, SPAN, HEADS), (0, 2, 1))
    row_index = lax.broadcasted_iota(jnp.int32, (SPAN, SPAN), 0)
    col_index = lax.broadcasted_iota(jnp.int32, (SPAN, SPAN), 1)
    unit_span = jnp.eye(SPAN, dtype=jnp.float32)

    def advance(carry_state, inputs):
        query_part, key_part, value_part, rate_part = inputs
        query_part = query_part.astype(jnp.float32)
        key_part = key_part.astype(jnp.float32)
        value_part = value_part.astype(jnp.float32)
        key_gram = jnp.einsum('hcd,hsd->hcs', key_part, key_part, precision=PRECISE)
        scores = jnp.einsum('hcd,hsd->hcs', query_part, key_part, precision=PRECISE)
        system = unit_span + jnp.where(col_index < row_index, rate_part[:, :, None] * key_gram, 0.0)
        right_side = rate_part[:, :, None] * jnp.concatenate((key_part, value_part), axis=-1)
        solved = jax.scipy.linalg.solve_triangular(system, right_side, lower=True, unit_diagonal=True)
        w_factor = solved[..., :KEY_SIZE]
        u_factor = solved[..., KEY_SIZE:]
        corrected = u_factor - jnp.einsum('hcd,hde->hce', w_factor, carry_state, precision=PRECISE)
        masked = jnp.where(col_index <= row_index, scores, 0.0)
        result = jnp.einsum('hcd,hde->hce', query_part, carry_state, precision=PRECISE)
        result = result + jnp.einsum('hcs,hse->hce', masked, corrected, precision=PRECISE)
        carry_state = carry_state + jnp.einsum('hcd,hce->hde', key_part, corrected, precision=PRECISE)
        return (carry_state, result)
    start_state = jnp.zeros((HEADS, KEY_SIZE, DV), jnp.float32)
    last_state, span_out = lax.scan(advance, start_state, (q_blocks, k_blocks, v_blocks, rate_blocks))
    mean_sq = lax.optimization_barrier(jnp.mean(span_out * span_out, axis=-1, keepdims=True))
    normed = span_out * lax.rsqrt(mean_sq + 1e-05) * out_gain
    return jnp.transpose(normed, (0, 2, 1, 3)).reshape(TOKEN_TOTAL, HEADS * DV).astype(jnp.bfloat16)
```

```python
import functools

import jax
import jax.numpy as jnp
from jax import lax
from jax.experimental import pallas as pl
from jax.experimental.pallas import tpu as pltpu
from jax.sharding import PartitionSpec as P

F32 = jnp.float32
BF16 = jnp.bfloat16
CHUNK = 128
RIM = 16
LEAD = 8
PAIR = 2
SMALL = 16
MESH = pl.DeviceIdType.MESH


def mm(a, b):
    return jnp.dot(a.astype(BF16), b.astype(BF16), preferred_element_type=F32)


def mm_nt(a, b):
    return lax.dot_general(a, b, (((1,), (1,)), ((), ())), preferred_element_type=F32)


def split(x):
    high = x.astype(BF16)
    return high, (x - high.astype(F32)).astype(BF16)


def local_kernel(taps, q_ref, k_ref, v_ref, rim_ref, w_ref, beta_ref,
                 a_ref, b_ref, lead_ref, known_ref, pad):
    step = pl.program_id(0)
    rows = q_ref.shape[0]
    dim = a_ref.shape[-1]
    chunks = rows // CHUNK
    row = lax.broadcasted_iota(jnp.int32, (CHUNK, CHUNK), 0)
    col = lax.broadcasted_iota(jnp.int32, (CHUNK, CHUNK), 1)
    head_lane = lax.broadcasted_iota(jnp.int32, beta_ref.shape, 1)
    zero = jnp.zeros((CHUNK, CHUNK), F32)

    def conv(which, ref, head):
        lanes = slice(head * dim, (head + 1) * dim)
        slot = head * 3 + which
        pad[slot, 0:LEAD] = rim_ref[which, RIM - LEAD:RIM, lanes].astype(F32)
        pad[slot, LEAD:] = ref[:, lanes].astype(F32)
        total = jnp.zeros((rows, dim), F32)
        for tap in range(taps):
            total = total + w_ref[which, tap:tap + 1, lanes] * pad[
                slot, pl.ds(LEAD - taps + 1 + tap, rows)]
        return total / (1.0 + jnp.exp(-total))

    qs, ks, vs, rates = [], [], [], []
    for head in range(PAIR):
        q = conv(0, q_ref, head).astype(BF16)
        k = conv(1, k_ref, head)
        k = (k * lax.rsqrt(jnp.sum(k * k, axis=-1, keepdims=True) + 1e-06)).astype(BF16)
        v = conv(2, v_ref, head).astype(BF16)
        rate = jnp.sum(
            jnp.where(head_lane == step * PAIR + head, beta_ref[...], 0.0), axis=1, keepdims=True)
        for c in range(chunks):
            part = slice(c * CHUNK, (c + 1) * CHUNK)
            qs.append(q[part])
            ks.append(k[part])
            vs.append(v[part])
            rates.append(rate[part])
    both = [mm_nt(jnp.concatenate((q, k), axis=0), k) for q, k in zip(qs, ks)]
    scores = [jnp.where(col <= row, x[:CHUNK], 0.0) for x in both]
    lower = [jnp.where(col < row, r * x[CHUNK:], 0.0) for r, x in zip(rates, both)]
    near = row // SMALL == col // SMALL
    power = [jnp.where(near, x, zero) for x in lower]
    rest = [-x for x in power]
    size = 2
    while size < SMALL:
        power = [mm(x, x) for x in power]
        rest = [x + y + mm(x, y) for x, y in zip(rest, power)]
        size *= 2
    size = SMALL
    while size < CHUNK:
        band = (row // (2 * size) == col // (2 * size)) & (row // size != col // size)
        off = [jnp.where(band, x, zero) for x in lower]
        mid = [x + mm(x, y) for x, y in zip(off, rest)]
        rest = [x - y - mm(x, y) for x, y in zip(rest, mid)]
        size *= 2
    flat = [jnp.sum(jnp.where(row == col, r, 0.0), axis=0, keepdims=True) for r in rates]
    kv = [jnp.concatenate((k, v), axis=1) for k, v in zip(ks, vs)]
    wu = [r * x.astype(F32) + mm(t * f, x) for r, x, t, f in zip(rates, kv, rest, flat)]
    made = [
        mm(jnp.concatenate((s, k.astype(F32).T), axis=0), x)
        for s, k, x in zip(scores, ks, wu)
    ]
    left = [
        jnp.concatenate((q.astype(F32) - x[:CHUNK, :dim], x[CHUNK:, :dim]), axis=0).astype(BF16)
        for q, x in zip(qs, made)
    ]
    eye = jnp.where(row == col, 1.0, 0.0)
    for c in range(chunks):
        part = slice(c * CHUNK, (c + 1) * CHUNK)
        for head in range(PAIR):
            n = head * chunks + c
            x = made[n]
            if c == 0:
                lead_ref[head, part] = left[n][:CHUNK]
                known_ref[head, part] = x[:CHUNK, dim:]
                a_ref[head] = eye - x[CHUNK:, :dim]
                b_ref[head] = x[CHUNK:, dim:]
            else:
                state = jnp.concatenate((a_ref[head], b_ref[head]), axis=1)
                y = mm(left[n], state)
                lead_ref[head, part] = y[:CHUNK, :dim].astype(BF16)
                known_ref[head, part] = y[:CHUNK, dim:] + x[:CHUNK, dim:]
                a_ref[head] = state[:, :dim] - y[CHUNK:, :dim]
                b_ref[head] = state[:, dim:] - y[CHUNK:, dim:] + x[CHUNK:, dim:]


def chain_kernel(seqs, blks, a_ref, b_ref, lead_ref, known_ref, gain_ref, o_ref,
                 came, goes, send_sem, recv_sem):
    heads, dim = a_ref.shape[0], a_ref.shape[-1]
    total = seqs * blks
    here = lax.axis_index("seq") * blks + lax.axis_index("blk")
    after = (here + 1) % total
    ahead = (here + total - 1) % total
    after_id = {"seq": after // blks, "blk": after % blks}
    ahead_id = {"seq": ahead // blks, "blk": ahead % blks}

    barrier = pltpu.get_barrier_semaphore()

    @pl.when(here > 0)
    def _():
        pl.semaphore_signal(barrier, inc=1, device_id=ahead_id, device_id_type=MESH)

    @pl.when(here < total - 1)
    def _():
        pl.semaphore_signal(barrier, inc=1, device_id=after_id, device_id_type=MESH)

    inner = (here > 0) & (here < total - 1)

    @pl.when(inner)
    def _():
        pl.semaphore_wait(barrier, 2)

    @pl.when(jnp.logical_not(inner))
    def _():
        pl.semaphore_wait(barrier, 1)

    def move(head):
        return pltpu.make_async_remote_copy(
            src_ref=goes.at[head], dst_ref=came.at[head],
            send_sem=send_sem.at[head], recv_sem=recv_sem.at[head],
            device_id=after_id, device_id_type=MESH)

    @pl.when(here == 0)
    def _():
        came[...] = jnp.zeros_like(came)

    def visit(head, carry):
        @pl.when(here > 0)
        def _():
            move(head).wait_recv()

        state_high, state_low = split(came[head])

        @pl.when(here < total - 1)
        def _():
            map_high, map_low = split(a_ref[head])
            goes[head] = b_ref[head] + (
                mm(map_high, state_high) + mm(map_high, state_low) + mm(map_low, state_high))
            move(head).start()

        out = known_ref[head] + mm(lead_ref[head], state_high)
        mean_sq = jnp.mean(out * out, axis=-1, keepdims=True)
        out = out * lax.rsqrt(mean_sq + 1e-05) * gain_ref[...]
        o_ref[:, pl.ds(pl.multiple_of(head * dim, dim), dim)] = out.astype(o_ref.dtype)
        return carry

    lax.fori_loop(0, heads, visit, 0)

    def close(head, carry):
        @pl.when(here < total - 1)
        def _():
            move(head).wait_send()
        return carry

    lax.fori_loop(0, heads, close, 0)


def on_device(query_raw, key_raw, value_raw, beta_rate, conv_weight, out_gain):
    rows, width = query_raw.shape
    heads = beta_rate.shape[1]
    dim = width // heads
    taps = conv_weight.shape[1]
    seqs, blks = lax.axis_size("seq"), lax.axis_size("blk")
    total = seqs * blks
    ends = jnp.stack([x[rows - RIM:] for x in (query_raw, key_raw, value_raw)])
    rim = lax.ppermute(ends, ("seq", "blk"), [(i, i + 1) for i in range(total - 1)])
    wide = PAIR * dim
    raw_spec = pl.BlockSpec((rows, wide), lambda i: (0, i))
    square = pl.BlockSpec((PAIR, dim, dim), lambda i: (i, 0, 0))
    tall = pl.BlockSpec((PAIR, rows, dim), lambda i: (i, 0, 0))
    maps, adds, lead, known = pl.pallas_call(
        functools.partial(local_kernel, taps),
        name="local_part",
        grid=(heads // PAIR,),
        out_shape=(
            jax.ShapeDtypeStruct((heads, dim, dim), F32),
            jax.ShapeDtypeStruct((heads, dim, dim), F32),
            jax.ShapeDtypeStruct((heads, rows, dim), BF16),
            jax.ShapeDtypeStruct((heads, rows, dim), F32),
        ),
        in_specs=[
            raw_spec, raw_spec, raw_spec,
            pl.BlockSpec((3, RIM, wide), lambda i: (0, 0, i)),
            pl.BlockSpec((3, taps, wide), lambda i: (0, 0, i)),
            pl.BlockSpec((rows, heads), lambda i: (0, 0)),
        ],
        out_specs=(square, square, tall, tall),
        scratch_shapes=[pltpu.VMEM((3 * PAIR, rows + LEAD, dim), F32)],
        compiler_params=pltpu.CompilerParams(vmem_limit_bytes=40 << 20),
    )(query_raw, key_raw, value_raw, rim, conv_weight, beta_rate)
    vmem = pl.BlockSpec(memory_space=pltpu.VMEM)
    return pl.pallas_call(
        functools.partial(chain_kernel, seqs, blks),
        name="chain_part",
        out_shape=jax.ShapeDtypeStruct((rows, width), BF16),
        in_specs=[vmem] * 5,
        out_specs=vmem,
        scratch_shapes=[
            pltpu.VMEM((heads, dim, dim), F32),
            pltpu.VMEM((heads, dim, dim), F32),
            pltpu.SemaphoreType.DMA((heads,)),
            pltpu.SemaphoreType.DMA((heads,)),
        ],
        compiler_params=pltpu.CompilerParams(
            collective_id=0, has_side_effects=True, vmem_limit_bytes=40 << 20),
    )(maps, adds, lead, known, out_gain.reshape(1, dim))


def solution(mesh):
    placed = (
        P(("groups", "seq", "blk"), "hd"),
        P(("groups", "seq", "blk"), "hd"),
        P(("groups", "seq", "blk"), "hd"),
        P(("groups", "seq", "blk"), "hd"),
        P(None, None, "hd"),
        P(),
    )
    return jax.shard_map(
        on_device,
        mesh=mesh,
        in_specs=placed,
        out_specs=P(("groups", "seq", "blk"), "hd"),
        check_vma=False,
    )
```

```python
import functools

import jax
import jax.numpy as jnp
from jax import lax
from jax.experimental import pallas as pl
from jax.experimental.pallas import tpu as pltpu
from jax.sharding import PartitionSpec as P

F32 = jnp.float32
BF16 = jnp.bfloat16
CHUNK = 128
RIM = 16
LEAD = 8
PAIR = 2
SMALL = 16
MESH = pl.DeviceIdType.MESH


def mm(a, b):
    return jnp.dot(a.astype(BF16), b.astype(BF16), preferred_element_type=F32)


def mm_nt(a, b):
    return lax.dot_general(a, b, (((1,), (1,)), ((), ())), preferred_element_type=F32)


def split(x):
    high = x.astype(BF16)
    return high, (x - high.astype(F32)).astype(BF16)


def mm3(a, b):
    a_high, a_low = split(a)
    b_high, b_low = split(b)
    return mm(a_high, b_high) + mm(a_high, b_low) + mm(a_low, b_high)


def layer_kernel(seqs, blks, taps, q_hbm, k_hbm, v_hbm, w_ref, beta_ref, gain_ref, o_ref,
                 raw, rim, pad, keys, wu_ref, state_ref, a_ref, b_ref, lead_ref, known_ref,
                 came, goes, load_sem, rim_send, rim_recv, send_sem, recv_sem):
    rows = q_hbm.shape[0]
    heads, dim = a_ref.shape[0], a_ref.shape[-1]
    chunks = rows // CHUNK
    pairs = heads // PAIR
    total = seqs * blks
    here = lax.axis_index("seq") * blks + lax.axis_index("blk")
    after = (here + 1) % total
    ahead = (here + total - 1) % total
    after_id = {"seq": after // blks, "blk": after % blks}
    ahead_id = {"seq": ahead // blks, "blk": ahead % blks}
    has_ahead = here > 0
    has_after = here < total - 1
    sources = (q_hbm, k_hbm, v_hbm)

    def load(which):
        return pltpu.make_async_copy(sources[which], raw.at[which], load_sem.at[which])

    def rim_move(which):
        return pltpu.make_async_remote_copy(
            src_ref=sources[which].at[pl.ds(rows - RIM, RIM)], dst_ref=rim.at[which],
            send_sem=rim_send.at[which], recv_sem=rim_recv.at[which],
            device_id=after_id, device_id_type=MESH)

    def move(head):
        return pltpu.make_async_remote_copy(
            src_ref=goes.at[head], dst_ref=came.at[head],
            send_sem=send_sem.at[head], recv_sem=recv_sem.at[head],
            device_id=after_id, device_id_type=MESH)

    barrier = pltpu.get_barrier_semaphore()

    @pl.when(has_ahead)
    def _():
        pl.semaphore_signal(barrier, inc=1, device_id=ahead_id, device_id_type=MESH)

    @pl.when(has_after)
    def _():
        pl.semaphore_signal(barrier, inc=1, device_id=after_id, device_id_type=MESH)

    for which in (1, 2, 0):
        load(which).start()

    @pl.when(here == 0)
    def _():
        came[...] = jnp.zeros_like(came)
        rim[...] = jnp.zeros_like(rim)

    inner = has_ahead & has_after

    @pl.when(inner)
    def _():
        pl.semaphore_wait(barrier, 2)

    @pl.when(jnp.logical_not(inner))
    def _():
        pl.semaphore_wait(barrier, 1)

    @pl.when(has_after)
    def _():
        for which in (1, 2, 0):
            rim_move(which).start()

    for which in (1, 2, 0):
        load(which).wait()

    @pl.when(has_ahead)
    def _():
        for which in (1, 2, 0):
            rim_move(which).wait_recv()

    row = lax.broadcasted_iota(jnp.int32, (CHUNK, CHUNK), 0)
    col = lax.broadcasted_iota(jnp.int32, (CHUNK, CHUNK), 1)
    head_lane = lax.broadcasted_iota(jnp.int32, beta_ref.shape, 1)
    eye = jnp.where(row == col, 1.0, 0.0)

    def lanes_of(head):
        return pl.ds(pl.multiple_of(head * dim, dim), dim)

    def conv(which, head, slot):
        lanes = lanes_of(head)
        pad[slot, 0:LEAD] = rim[which, RIM - LEAD:RIM, lanes].astype(F32)
        pad[slot, LEAD:] = raw[which, :, lanes].astype(F32)
        summed = jnp.zeros((rows, dim), F32)
        for tap in range(taps):
            summed = summed + w_ref[which, tap:tap + 1, lanes] * pad[
                slot, pl.ds(LEAD - taps + 1 + tap, rows)]
        return summed / (1.0 + jnp.exp(-summed))

    def maps_of(pair):
        ks, vs, rates = [], [], []
        for lane in range(PAIR):
            head = pair * PAIR + lane
            k = conv(1, head, lane * 2)
            k = (k * lax.rsqrt(jnp.sum(k * k, axis=-1, keepdims=True) + 1e-06)).astype(BF16)
            keys[:, lanes_of(head)] = k
            v = conv(2, head, lane * 2 + 1).astype(BF16)
            rate = jnp.sum(
                jnp.where(head_lane == head, beta_ref[...], 0.0), axis=1, keepdims=True)
            for c in range(chunks):
                part = slice(c * CHUNK, (c + 1) * CHUNK)
                ks.append(k[part])
                vs.append(v[part])
                rates.append(rate[part])
        lower = [jnp.where(col < row, r * mm_nt(k, k), 0.0) for r, k in zip(rates, ks)]
        near = row // SMALL == col // SMALL
        power = [jnp.where(near, x, 0.0) for x in lower]
        rest = [-x for x in power]
        size = 2
        while size < SMALL:
            power = [mm(x, x) for x in power]
            rest = [x + y + mm(x, y) for x, y in zip(rest, power)]
            size *= 2
        size = SMALL
        while size < CHUNK:
            band = (row // (2 * size) == col // (2 * size)) & (row // size != col // size)
            off = [jnp.where(band, x, 0.0) for x in lower]
            mid = [x + mm(x, y) for x, y in zip(off, rest)]
            rest = [x - y - mm(x, y) for x, y in zip(rest, mid)]
            size *= 2
        flat = [jnp.sum(jnp.where(row == col, r, 0.0), axis=0, keepdims=True) for r in rates]
        kv = [jnp.concatenate((k, v), axis=1) for k, v in zip(ks, vs)]
        wu = [r * x.astype(F32) + mm(t * f, x) for r, x, t, f in zip(rates, kv, rest, flat)]
        made = []
        for k, x in zip(ks, wu):
            turned = k.astype(F32).T.astype(BF16)
            high, low = split(x)
            made.append(mm(turned, high) + mm(turned, low))
        states = [jnp.concatenate((eye, jnp.zeros((dim, dim), F32)), axis=1)] * PAIR
        for c in range(chunks):
            part = slice(c * CHUNK, (c + 1) * CHUNK)
            for lane in range(PAIR):
                head = pair * PAIR + lane
                x = made[lane * chunks + c]
                wu_ref[head, part] = wu[lane * chunks + c]
                state_ref[head, part] = states[lane]
                step = x[:, :dim] if c else None
                written = jnp.concatenate((jnp.zeros((dim, dim), F32), x[:, dim:]), axis=1)
                if c:
                    states[lane] = states[lane] - mm(step, states[lane]) + written
                else:
                    states[lane] = jnp.concatenate((eye - x[:, :dim], x[:, dim:]), axis=1)
        for lane in range(PAIR):
            a_ref[pair * PAIR + lane] = states[lane][:, :dim]
            b_ref[pair * PAIR + lane] = states[lane][:, dim:]

    def pass_on(pair):
        for lane in range(PAIR):
            head = pair * PAIR + lane

            @pl.when(has_ahead)
            def _():
                move(head).wait_recv()

            @pl.when(has_after)
            def _():
                map_high, map_low = split(a_ref[head])
                state = came[head]
                goes[head] = (b_ref[head] + (mm(map_high, state) + mm(map_low, state))).astype(BF16)
                move(head).start()

    def reads_of(pair):
        for lane in range(PAIR):
            head = pair * PAIR + lane
            q = conv(0, head, lane).astype(BF16)
            for c in range(chunks):
                part = slice(c * CHUNK, (c + 1) * CHUNK)
                scores = jnp.where(col <= row, mm_nt(q[part], keys[part, lanes_of(head)]), 0.0)
                near = mm3(scores, wu_ref[head, part])
                y = mm3(q[part].astype(F32) - near[:, :dim], state_ref[head, part])
                lead_ref[head, part] = y[:, :dim]
                known_ref[head, part] = y[:, dim:] + near[:, dim:]

    def finish(pair):
        for lane in range(PAIR):
            head = pair * PAIR + lane
            high, low = split(lead_ref[head])
            state = came[head]
            out = known_ref[head] + (mm(high, state) + mm(low, state))
            mean_sq = jnp.mean(out * out, axis=-1, keepdims=True)
            out = out * lax.rsqrt(mean_sq + 1e-05) * gain_ref[...]
            o_ref[:, lanes_of(head)] = out.astype(o_ref.dtype)

    def first_part(i, carry):
        maps_of(i)

        @pl.when(i >= here)
        def _():
            pass_on(i - here)
        return carry

    def second_part(i, carry):
        reads_of(i - pairs)

        @pl.when((i >= here) & (i < here + pairs))
        def _():
            pass_on(i - here)

        @pl.when(here <= pairs)
        def _():
            finish(i - pairs)

        @pl.when((here > pairs) & (i >= here))
        def _():
            finish(i - here)
        return carry

    def third_part(i, carry):
        @pl.when(i >= here)
        def _():
            pass_on(i - here)
            finish(i - here)
        return carry

    lax.fori_loop(0, pairs, first_part, 0)
    lax.fori_loop(pairs, 2 * pairs, second_part, 0)
    lax.fori_loop(2 * pairs, here + pairs, third_part, 0)

    @pl.when(has_after)
    def _():
        for which in range(3):
            rim_move(which).wait_send()
        for head in range(heads):
            move(head).wait_send()


def on_device(query_raw, key_raw, value_raw, beta_rate, conv_weight, out_gain):
    rows, width = query_raw.shape
    heads = beta_rate.shape[1]
    dim = width // heads
    taps = conv_weight.shape[1]
    seqs, blks = lax.axis_size("seq"), lax.axis_size("blk")
    far = pl.BlockSpec(memory_space=pltpu.HBM)
    vmem = pl.BlockSpec(memory_space=pltpu.VMEM)
    return pl.pallas_call(
        functools.partial(layer_kernel, seqs, blks, taps),
        name="layer",
        out_shape=jax.ShapeDtypeStruct((rows, width), BF16),
        in_specs=[far, far, far, vmem, vmem, vmem],
        out_specs=vmem,
        scratch_shapes=[
            pltpu.VMEM((3, rows, width), BF16),
            pltpu.VMEM((3, RIM, width), BF16),
            pltpu.VMEM((2 * PAIR, rows + LEAD, dim), F32),
            pltpu.VMEM((rows, width), BF16),
            pltpu.VMEM((heads, rows, 2 * dim), F32),
            pltpu.VMEM((heads, rows, 2 * dim), F32),
            pltpu.VMEM((heads, dim, dim), F32),
            pltpu.VMEM((heads, dim, dim), F32),
            pltpu.VMEM((heads, rows, dim), F32),
            pltpu.VMEM((heads, rows, dim), F32),
            pltpu.VMEM((heads, dim, dim), BF16),
            pltpu.VMEM((heads, dim, dim), BF16),
            pltpu.SemaphoreType.DMA((3,)),
            pltpu.SemaphoreType.DMA((3,)),
            pltpu.SemaphoreType.DMA((3,)),
            pltpu.SemaphoreType.DMA((heads,)),
            pltpu.SemaphoreType.DMA((heads,)),
        ],
        compiler_params=pltpu.CompilerParams(
            collective_id=0, has_side_effects=True, vmem_limit_bytes=56 << 20),
    )(query_raw, key_raw, value_raw, conv_weight, beta_rate, out_gain.reshape(1, dim))


def solution(mesh):
    placed = (
        P(("groups", "seq", "blk"), "hd"),
        P(("groups", "seq", "blk"), "hd"),
        P(("groups", "seq", "blk"), "hd"),
        P(("groups", "seq", "blk"), "hd"),
        P(None, None, "hd"),
        P(),
    )
    return jax.shard_map(
        on_device,
        mesh=mesh,
        in_specs=placed,
        out_specs=P(("groups", "seq", "blk"), "hd"),
        check_vma=False,
    )
```

```python
import functools

import jax
import jax.numpy as jnp
from jax import lax
from jax.experimental import pallas as pl
from jax.experimental.pallas import tpu as pltpu
from jax.sharding import PartitionSpec as P

F32 = jnp.float32
BF16 = jnp.bfloat16
CHUNK = 128
RIM = 16
LEAD = 8
PAIR = 2
SMALL = 16
MESH = pl.DeviceIdType.MESH


def mm(a, b):
    return jnp.dot(a.astype(BF16), b.astype(BF16), preferred_element_type=F32)


def mm_nt(a, b):
    return lax.dot_general(a, b, (((1,), (1,)), ((), ())), preferred_element_type=F32)


def split(x):
    high = x.astype(BF16)
    return high, (x - high.astype(F32)).astype(BF16)


def mm3(a, b):
    a_high, a_low = split(a)
    b_high, b_low = split(b)
    return mm(a_high, b_high) + mm(a_high, b_low) + mm(a_low, b_high)


def layer_kernel(seqs, blks, taps, q_hbm, k_hbm, v_hbm, w_ref, beta_ref, gain_ref, o_ref,
                 raw, rim, pad, keys, wu_ref, state_ref, a_ref, b_ref, lead_ref, known_ref,
                 came, goes, load_sem, rim_send, rim_recv, send_sem, recv_sem):
    rows = q_hbm.shape[0]
    heads, dim = b_ref.shape[0], b_ref.shape[-1]
    chunks = rows // CHUNK
    pairs = heads // PAIR
    total = seqs * blks
    here = lax.axis_index("seq") * blks + lax.axis_index("blk")
    after = (here + 1) % total
    ahead = (here + total - 1) % total
    after_id = {"seq": after // blks, "blk": after % blks}
    ahead_id = {"seq": ahead // blks, "blk": ahead % blks}
    has_ahead = here > 0
    has_after = here < total - 1
    sources = (q_hbm, k_hbm, v_hbm)

    def load(which):
        return pltpu.make_async_copy(sources[which], raw.at[which], load_sem.at[which])

    def rim_move(which):
        return pltpu.make_async_remote_copy(
            src_ref=sources[which].at[pl.ds(rows - RIM, RIM)], dst_ref=rim.at[which],
            send_sem=rim_send.at[which], recv_sem=rim_recv.at[which],
            device_id=after_id, device_id_type=MESH)

    def move(head):
        return pltpu.make_async_remote_copy(
            src_ref=goes.at[head], dst_ref=came.at[head],
            send_sem=send_sem.at[head], recv_sem=recv_sem.at[head],
            device_id=after_id, device_id_type=MESH)

    barrier = pltpu.get_barrier_semaphore()

    @pl.when(has_ahead)
    def _():
        pl.semaphore_signal(barrier, inc=1, device_id=ahead_id, device_id_type=MESH)

    @pl.when(has_after)
    def _():
        pl.semaphore_signal(barrier, inc=1, device_id=after_id, device_id_type=MESH)

    for which in (1, 2, 0):
        load(which).start()

    @pl.when(here == 0)
    def _():
        came[...] = jnp.zeros_like(came)
        rim[...] = jnp.zeros_like(rim)

    inner = has_ahead & has_after

    @pl.when(inner)
    def _():
        pl.semaphore_wait(barrier, 2)

    @pl.when(jnp.logical_not(inner))
    def _():
        pl.semaphore_wait(barrier, 1)

    @pl.when(has_after)
    def _():
        for which in (1, 2, 0):
            rim_move(which).start()

    def arrive(which):
        load(which).wait()

        @pl.when(has_ahead)
        def _():
            rim_move(which).wait_recv()

    arrive(1)
    arrive(2)

    row = lax.broadcasted_iota(jnp.int32, (CHUNK, CHUNK), 0)
    col = lax.broadcasted_iota(jnp.int32, (CHUNK, CHUNK), 1)
    head_row = lax.broadcasted_iota(jnp.int32, (heads, CHUNK), 0)
    eye = jnp.where(row == col, 1.0, 0.0)

    def lanes_of(head):
        return pl.ds(pl.multiple_of(head * dim, dim), dim)

    def conv(which, head, slot):
        lanes = lanes_of(head)
        pad[slot, 0:LEAD] = rim[which, RIM - LEAD:RIM, lanes].astype(F32)
        pad[slot, LEAD:] = raw[which, :, lanes].astype(F32)
        summed = jnp.zeros((rows, dim), F32)
        for tap in range(taps):
            summed = summed + w_ref[which, tap:tap + 1, lanes] * pad[
                slot, pl.ds(LEAD - taps + 1 + tap, rows)]
        half = 0.5 * summed
        return half + half * jnp.tanh(half)

    def maps_of(pair):
        ks, vs, rates, flat = [], [], [], []
        for lane in range(PAIR):
            head = pair * PAIR + lane
            k = conv(1, head, lane * 2)
            k = (k * lax.rsqrt(jnp.sum(k * k, axis=-1, keepdims=True) + 1e-06)).astype(BF16)
            keys[:, lanes_of(head)] = k
            v = conv(2, head, lane * 2 + 1).astype(BF16)
            for c in range(chunks):
                part = slice(c * CHUNK, (c + 1) * CHUNK)
                ks.append(k[part])
                vs.append(v[part])
                flat.append(jnp.sum(jnp.where(head_row == head, beta_ref[:, part], 0.0), axis=0, keepdims=True))
                rates.append(jnp.sum(jnp.where(row == col, flat[-1], 0.0), axis=1, keepdims=True))
        lower = [jnp.where(col < row, r * mm_nt(k, k), 0.0) for r, k in zip(rates, ks)]
        near = row // SMALL == col // SMALL
        power = [jnp.where(near, x, 0.0) for x in lower]
        rest = [-x for x in power]
        power = [mm(x, x) for x in power]
        size = 4
        while size < SMALL:
            joint = [mm(jnp.concatenate((x, y), axis=0), y) for x, y in zip(rest, power)]
            rest = [x + y + z[:CHUNK] for x, y, z in zip(rest, power, joint)]
            power = [z[CHUNK:] for z in joint]
            size *= 2
        rest = [x + y + mm(x, y) for x, y in zip(rest, power)]
        size = SMALL
        while size < CHUNK:
            band = (row // (2 * size) == col // (2 * size)) & (row // size != col // size)
            off = [jnp.where(band, x, 0.0) for x in lower]
            mid = [x + mm(x, y) for x, y in zip(off, rest)]
            rest = [x - y - mm(x, y) for x, y in zip(rest, mid)]
            size *= 2
        kv = [jnp.concatenate((k, v), axis=1) for k, v in zip(ks, vs)]
        wu = [r * x.astype(F32) + mm(t * f, x) for r, x, t, f in zip(rates, kv, rest, flat)]
        made = []
        for k, x in zip(ks, wu):
            turned = k.astype(F32).T.astype(BF16)
            made.append(mm(jnp.concatenate((turned, turned), axis=1),
                           jnp.concatenate(split(x), axis=0)))
        states = [jnp.concatenate((eye, jnp.zeros((dim, dim), F32)), axis=1)] * PAIR
        for c in range(chunks):
            part = slice(c * CHUNK, (c + 1) * CHUNK)
            for lane in range(PAIR):
                head = pair * PAIR + lane
                x = made[lane * chunks + c]
                wu_ref[head, part] = wu[lane * chunks + c]
                state_ref[head, part] = states[lane]
                step = x[:, :dim] if c else None
                written = jnp.concatenate((jnp.zeros((dim, dim), F32), x[:, dim:]), axis=1)
                if c:
                    states[lane] = states[lane] - mm(step, states[lane]) + written
                else:
                    states[lane] = jnp.concatenate((eye - x[:, :dim], x[:, dim:]), axis=1)
        for lane in range(PAIR):
            a_ref[pair * PAIR + lane] = jnp.concatenate(split(states[lane][:, :dim]), axis=1)
            b_ref[pair * PAIR + lane] = states[lane][:, dim:]

    def pass_on(pair):
        for lane in range(PAIR):
            head = pair * PAIR + lane

            @pl.when(has_ahead)
            def _():
                move(head).wait_recv()

            @pl.when(has_after)
            def _():
                state = came[head]
                goes[head] = (
                    b_ref[head] + mm(a_ref[head], jnp.concatenate((state, state), axis=0))
                ).astype(BF16)
                move(head).start()

    def reads_of(pair):
        for lane in range(PAIR):
            head = pair * PAIR + lane
            q = conv(0, head, lane).astype(BF16)
            for c in range(chunks):
                part = slice(c * CHUNK, (c + 1) * CHUNK)
                scores = jnp.where(col <= row, mm_nt(q[part], keys[part, lanes_of(head)]), 0.0)
                near = mm3(scores, wu_ref[head, part])
                y = mm3(q[part].astype(F32) - near[:, :dim], state_ref[head, part])
                lead_ref[head, part] = y[:, :dim]
                known_ref[head, part] = y[:, dim:] + near[:, dim:]

    def finish(pair):
        for lane in range(PAIR):
            head = pair * PAIR + lane
            state = came[head]
            out = known_ref[head] + mm(
                jnp.concatenate(split(lead_ref[head]), axis=1),
                jnp.concatenate((state, state), axis=0))
            mean_sq = jnp.mean(out * out, axis=-1, keepdims=True)
            out = out * lax.rsqrt(mean_sq + 1e-05) * gain_ref[...]
            o_ref[:, lanes_of(head)] = out.astype(o_ref.dtype)

    def first_part(i, carry):
        maps_of(i)

        @pl.when(i >= here)
        def _():
            pass_on(i - here)
        return carry

    def second_part(i, carry):
        reads_of(i - pairs)

        @pl.when((i >= here) & (i < here + pairs))
        def _():
            pass_on(i - here)

        @pl.when(here <= pairs)
        def _():
            finish(i - pairs)

        @pl.when((here > pairs) & (i >= here))
        def _():
            finish(i - here)
        return carry

    def third_part(i, carry):
        @pl.when(i >= here)
        def _():
            pass_on(i - here)
            finish(i - here)
        return carry

    lax.fori_loop(0, pairs, first_part, 0)
    arrive(0)
    lax.fori_loop(pairs, 2 * pairs, second_part, 0)
    lax.fori_loop(2 * pairs, here + pairs, third_part, 0)

    @pl.when(has_after)
    def _():
        for which in range(3):
            rim_move(which).wait_send()
        for head in range(heads):
            move(head).wait_send()


def on_device(query_raw, key_raw, value_raw, beta_rate, conv_weight, out_gain):
    rows, width = query_raw.shape
    heads = beta_rate.shape[1]
    dim = width // heads
    taps = conv_weight.shape[1]
    seqs, blks = lax.axis_size("seq"), lax.axis_size("blk")
    far = pl.BlockSpec(memory_space=pltpu.HBM)
    vmem = pl.BlockSpec(memory_space=pltpu.VMEM)
    return pl.pallas_call(
        functools.partial(layer_kernel, seqs, blks, taps),
        name="layer",
        out_shape=jax.ShapeDtypeStruct((rows, width), BF16),
        in_specs=[far, far, far, vmem, vmem, vmem],
        out_specs=vmem,
        scratch_shapes=[
            pltpu.VMEM((3, rows, width), BF16),
            pltpu.VMEM((3, RIM, width), BF16),
            pltpu.VMEM((2 * PAIR, rows + LEAD, dim), F32),
            pltpu.VMEM((rows, width), BF16),
            pltpu.VMEM((heads, rows, 2 * dim), F32),
            pltpu.VMEM((heads, rows, 2 * dim), F32),
            pltpu.VMEM((heads, dim, 2 * dim), BF16),
            pltpu.VMEM((heads, dim, dim), F32),
            pltpu.VMEM((heads, rows, dim), F32),
            pltpu.VMEM((heads, rows, dim), F32),
            pltpu.VMEM((heads, dim, dim), BF16),
            pltpu.VMEM((heads, dim, dim), BF16),
            pltpu.SemaphoreType.DMA((3,)),
            pltpu.SemaphoreType.DMA((3,)),
            pltpu.SemaphoreType.DMA((3,)),
            pltpu.SemaphoreType.DMA((heads,)),
            pltpu.SemaphoreType.DMA((heads,)),
        ],
        compiler_params=pltpu.CompilerParams(
            collective_id=0, has_side_effects=True, vmem_limit_bytes=56 << 20),
    )(query_raw, key_raw, value_raw, conv_weight, beta_rate.T, out_gain.reshape(1, dim))


def solution(mesh):
    placed = (
        P(("groups", "seq", "blk"), "hd"),
        P(("groups", "seq", "blk"), "hd"),
        P(("groups", "seq", "blk"), "hd"),
        P(("groups", "seq", "blk"), "hd"),
        P(None, None, "hd"),
        P(),
    )
    return jax.shard_map(
        on_device,
        mesh=mesh,
        in_specs=placed,
        out_specs=P(("groups", "seq", "blk"), "hd"),
        check_vma=False,
    )
```

```python
import functools

import jax
import jax.numpy as jnp
from jax import lax
from jax.experimental import pallas as pl
from jax.experimental.pallas import tpu as pltpu
from jax.sharding import PartitionSpec as P

F32 = jnp.float32
BF16 = jnp.bfloat16
CHUNK = 128
RIM = 16
LEAD = 8
PAIR = 2
SMALL = 16
MESH = pl.DeviceIdType.MESH


def mm(a, b):
    return jnp.dot(a.astype(BF16), b.astype(BF16), preferred_element_type=F32)


def mm_nt(a, b):
    return lax.dot_general(a, b, (((1,), (1,)), ((), ())), preferred_element_type=F32)


def split(x):
    high = x.astype(BF16)
    return high, (x - high.astype(F32)).astype(BF16)


def mm3(a, b):
    a_high, a_low = split(a)
    b_high, b_low = split(b)
    return mm(a_high, b_high) + mm(a_high, b_low) + mm(a_low, b_high)


def layer_kernel(seqs, blks, taps, q_hbm, k_hbm, v_hbm, w_ref, beta_ref, gain_ref, o_ref,
                 raw, rim, pad, keys, wu_ref, state_ref, a_ref, b_ref, lead_ref, known_ref,
                 came, goes, before, onward, row_a, row_b, load_sem, rim_send, rim_recv,
                 join_send, join_recv, send_sem, recv_sem):
    rows = q_hbm.shape[0]
    heads, dim = b_ref.shape[0], b_ref.shape[-1]
    chunks = rows // CHUNK
    pairs = heads // PAIR
    total = seqs * blks
    z, x = lax.axis_index("seq"), lax.axis_index("blk")
    end = blks - 1
    here = z * blks + x
    lag = z + end
    sends_row = x < end
    sends_state = (x == end) & (z < seqs - 1)
    below = (z + 1) % seqs
    after = (here + 1) % total
    ahead = (here + total - 1) % total
    after_id = {"seq": after // blks, "blk": after % blks}
    ahead_id = {"seq": ahead // blks, "blk": ahead % blks}
    has_ahead = here > 0
    has_after = here < total - 1
    sources = (q_hbm, k_hbm, v_hbm)

    def load(which):
        return pltpu.make_async_copy(sources[which], raw.at[which], load_sem.at[which])

    def rim_move(which):
        return pltpu.make_async_remote_copy(
            src_ref=sources[which].at[pl.ds(rows - RIM, RIM)], dst_ref=rim.at[which],
            send_sem=rim_send.at[which], recv_sem=rim_recv.at[which],
            device_id=after_id, device_id_type=MESH)

    def join(head):
        return pltpu.make_async_remote_copy(
            src_ref=onward.at[head], dst_ref=before.at[head],
            send_sem=join_send.at[head], recv_sem=join_recv.at[head],
            device_id={"seq": z, "blk": (x + 1) % blks}, device_id_type=MESH)

    def move(head, target):
        return pltpu.make_async_remote_copy(
            src_ref=goes.at[head], dst_ref=came.at[head],
            send_sem=send_sem.at[target, head], recv_sem=recv_sem.at[head],
            device_id={"seq": below, "blk": target}, device_id_type=MESH)

    barrier = pltpu.get_barrier_semaphore()

    @pl.when(has_ahead)
    def _():
        pl.semaphore_signal(barrier, inc=1, device_id=ahead_id, device_id_type=MESH)

    @pl.when(has_after)
    def _():
        pl.semaphore_signal(barrier, inc=1, device_id=after_id, device_id_type=MESH)

    for which in (1, 2, 0):
        load(which).start()

    @pl.when(here == 0)
    def _():
        rim[...] = jnp.zeros_like(rim)

    @pl.when(z == 0)
    def _():
        came[...] = jnp.zeros_like(came)

    extra_up = (x > 0) & (z > 0)

    @pl.when(extra_up)
    def _():
        pl.semaphore_signal(barrier, inc=1, device_id={"seq": (z + seqs - 1) % seqs, "blk": end},
                            device_id_type=MESH)

    @pl.when(sends_state)
    def _():
        for target in range(1, blks):
            pl.semaphore_signal(barrier, inc=1, device_id={"seq": below, "blk": target},
                                device_id_type=MESH)

    pl.semaphore_wait(
        barrier,
        has_ahead.astype(jnp.int32) + has_after.astype(jnp.int32)
        + extra_up.astype(jnp.int32) + end * sends_state.astype(jnp.int32))

    @pl.when(has_after)
    def _():
        for which in (1, 2, 0):
            rim_move(which).start()

    def arrive(which):
        load(which).wait()

        @pl.when(has_ahead)
        def _():
            rim_move(which).wait_recv()

    arrive(1)
    arrive(2)

    row = lax.broadcasted_iota(jnp.int32, (CHUNK, CHUNK), 0)
    col = lax.broadcasted_iota(jnp.int32, (CHUNK, CHUNK), 1)
    head_row = lax.broadcasted_iota(jnp.int32, (heads, CHUNK), 0)
    eye = jnp.where(row == col, 1.0, 0.0)

    @pl.when(x == 0)
    def _():
        for head in range(heads):
            before[head] = jnp.concatenate((eye, jnp.zeros_like(eye)), axis=1).astype(BF16)

    def lanes_of(head):
        return pl.ds(pl.multiple_of(head * dim, dim), dim)

    def conv(which, head, slot):
        lanes = lanes_of(head)
        pad[slot, 0:LEAD] = rim[which, RIM - LEAD:RIM, lanes].astype(F32)
        pad[slot, LEAD:] = raw[which, :, lanes].astype(F32)
        summed = jnp.zeros((rows, dim), F32)
        for tap in range(taps):
            summed = summed + w_ref[which, tap:tap + 1, lanes] * pad[
                slot, pl.ds(LEAD - taps + 1 + tap, rows)]
        half = 0.5 * summed
        return half + half * jnp.tanh(half)

    def maps_of(pair):
        ks, vs, rates, flat = [], [], [], []
        for lane in range(PAIR):
            head = pair * PAIR + lane
            k = conv(1, head, lane * 2)
            k = (k * lax.rsqrt(jnp.sum(k * k, axis=-1, keepdims=True) + 1e-06)).astype(BF16)
            keys[:, lanes_of(head)] = k
            v = conv(2, head, lane * 2 + 1).astype(BF16)
            for c in range(chunks):
                part = slice(c * CHUNK, (c + 1) * CHUNK)
                ks.append(k[part])
                vs.append(v[part])
                flat.append(jnp.sum(jnp.where(head_row == head, beta_ref[:, part], 0.0), axis=0, keepdims=True))
                rates.append(jnp.sum(jnp.where(row == col, flat[-1], 0.0), axis=1, keepdims=True))
        lower = [jnp.where(col < row, r * mm_nt(k, k), 0.0) for r, k in zip(rates, ks)]
        near = row // SMALL == col // SMALL
        power = [jnp.where(near, x, 0.0) for x in lower]
        rest = [-x for x in power]
        power = [mm(x, x) for x in power]
        size = 4
        while size < SMALL:
            joint = [mm(jnp.concatenate((x, y), axis=0), y) for x, y in zip(rest, power)]
            rest = [x + y + z[:CHUNK] for x, y, z in zip(rest, power, joint)]
            power = [z[CHUNK:] for z in joint]
            size *= 2
        rest = [x + y + mm(x, y) for x, y in zip(rest, power)]
        size = SMALL
        while size < CHUNK:
            band = (row // (2 * size) == col // (2 * size)) & (row // size != col // size)
            off = [jnp.where(band, x, 0.0) for x in lower]
            mid = [x + mm(x, y) for x, y in zip(off, rest)]
            rest = [x - y - mm(x, y) for x, y in zip(rest, mid)]
            size *= 2
        kv = [jnp.concatenate((k, v), axis=1) for k, v in zip(ks, vs)]
        wu = [r * x.astype(F32) + mm(t * f, x) for r, x, t, f in zip(rates, kv, rest, flat)]
        made = []
        for k, solved in zip(ks, wu):
            turned = k.astype(F32).T.astype(BF16)
            made.append(mm(jnp.concatenate((turned, turned), axis=1),
                           jnp.concatenate(split(solved), axis=0)))
        states = [jnp.concatenate((eye, jnp.zeros((dim, dim), F32)), axis=1)] * PAIR
        for c in range(chunks):
            part = slice(c * CHUNK, (c + 1) * CHUNK)
            for lane in range(PAIR):
                head = pair * PAIR + lane
                x = made[lane * chunks + c]
                wu_ref[head, part] = wu[lane * chunks + c]
                state_ref[head, part] = states[lane]
                step = x[:, :dim] if c else None
                written = jnp.concatenate((jnp.zeros((dim, dim), F32), x[:, dim:]), axis=1)
                if c:
                    states[lane] = states[lane] - mm(step, states[lane]) + written
                else:
                    states[lane] = jnp.concatenate((eye - x[:, :dim], x[:, dim:]), axis=1)
        for lane in range(PAIR):
            a_ref[pair * PAIR + lane] = jnp.concatenate(split(states[lane][:, :dim]), axis=1)
            b_ref[pair * PAIR + lane] = states[lane][:, dim:]

    def compose(pair):
        for lane in range(PAIR):
            head = pair * PAIR + lane

            @pl.when(x > 0)
            def _():
                join(head).wait_recv()

            prior = before[head]
            both = mm(a_ref[head], jnp.concatenate((prior, prior), axis=0))
            made_map, made_add = both[:, :dim], both[:, dim:] + b_ref[head]

            @pl.when(sends_row)
            def _():
                onward[head] = jnp.concatenate((made_map, made_add), axis=1).astype(BF16)
                join(head).start()

            @pl.when(sends_state)
            def _():
                row_a[head] = jnp.concatenate(split(made_map), axis=1)
                row_b[head] = made_add

    def pass_on(pair):
        for lane in range(PAIR):
            head = pair * PAIR + lane

            @pl.when(z > 0)
            def _():
                move(head, 0).wait_recv()

            @pl.when(sends_state)
            def _():
                state = came[head]
                goes[head] = (
                    row_b[head] + mm(row_a[head], jnp.concatenate((state, state), axis=0))
                ).astype(BF16)
                for target in range(blks - 1, -1, -1):
                    move(head, target).start()

    def reads_of(pair):
        for lane in range(PAIR):
            head = pair * PAIR + lane
            q = conv(0, head, lane).astype(BF16)
            for c in range(chunks):
                part = slice(c * CHUNK, (c + 1) * CHUNK)
                scores = jnp.where(col <= row, mm_nt(q[part], keys[part, lanes_of(head)]), 0.0)
                near = mm3(scores, wu_ref[head, part])
                y = mm3(q[part].astype(F32) - near[:, :dim], state_ref[head, part])
                lead_ref[head, part] = y[:, :dim]
                known_ref[head, part] = y[:, dim:] + near[:, dim:]

    def finish(pair):
        for lane in range(PAIR):
            head = pair * PAIR + lane
            prior = before[head]
            state = (mm(prior[:, :dim], came[head]) + prior[:, dim:].astype(F32)).astype(BF16)
            out = known_ref[head] + mm(
                jnp.concatenate(split(lead_ref[head]), axis=1),
                jnp.concatenate((state, state), axis=0))
            mean_sq = jnp.mean(out * out, axis=-1, keepdims=True)
            out = out * lax.rsqrt(mean_sq + 1e-05) * gain_ref[...]
            o_ref[:, lanes_of(head)] = out.astype(o_ref.dtype)

    def first_part(i, carry):
        maps_of(i)

        @pl.when((i >= x) & (i < x + pairs))
        def _():
            compose(i - x)

        @pl.when(i >= lag)
        def _():
            pass_on(i - lag)
        return carry

    def second_part(i, carry):
        reads_of(i - pairs)

        @pl.when((i >= x) & (i < x + pairs))
        def _():
            compose(i - x)

        @pl.when((i >= lag) & (i < lag + pairs))
        def _():
            pass_on(i - lag)

        @pl.when(lag <= pairs)
        def _():
            finish(i - pairs)

        @pl.when((lag > pairs) & (i >= lag))
        def _():
            finish(i - lag)
        return carry

    def third_part(i, carry):
        @pl.when((i >= x) & (i < x + pairs))
        def _():
            compose(i - x)

        @pl.when(i >= lag)
        def _():
            pass_on(i - lag)
            finish(i - lag)
        return carry

    lax.fori_loop(0, pairs, first_part, 0)
    arrive(0)
    lax.fori_loop(pairs, 2 * pairs, second_part, 0)
    lax.fori_loop(2 * pairs, lag + pairs, third_part, 0)

    @pl.when(has_after)
    def _():
        for which in range(3):
            rim_move(which).wait_send()

    @pl.when(sends_row)
    def _():
        for head in range(heads):
            join(head).wait_send()

    @pl.when(sends_state)
    def _():
        for head in range(heads):
            for target in range(blks):
                move(head, target).wait_send()


def on_device(query_raw, key_raw, value_raw, beta_rate, conv_weight, out_gain):
    rows, width = query_raw.shape
    heads = beta_rate.shape[1]
    dim = width // heads
    taps = conv_weight.shape[1]
    seqs, blks = lax.axis_size("seq"), lax.axis_size("blk")
    far = pl.BlockSpec(memory_space=pltpu.HBM)
    vmem = pl.BlockSpec(memory_space=pltpu.VMEM)
    return pl.pallas_call(
        functools.partial(layer_kernel, seqs, blks, taps),
        name="layer",
        out_shape=jax.ShapeDtypeStruct((rows, width), BF16),
        in_specs=[far, far, far, vmem, vmem, vmem],
        out_specs=vmem,
        scratch_shapes=[
            pltpu.VMEM((3, rows, width), BF16),
            pltpu.VMEM((3, RIM, width), BF16),
            pltpu.VMEM((2 * PAIR, rows + LEAD, dim), F32),
            pltpu.VMEM((rows, width), BF16),
            pltpu.VMEM((heads, rows, 2 * dim), F32),
            pltpu.VMEM((heads, rows, 2 * dim), F32),
            pltpu.VMEM((heads, dim, 2 * dim), BF16),
            pltpu.VMEM((heads, dim, dim), F32),
            pltpu.VMEM((heads, rows, dim), F32),
            pltpu.VMEM((heads, rows, dim), F32),
            pltpu.VMEM((heads, dim, dim), BF16),
            pltpu.VMEM((heads, dim, dim), BF16),
            pltpu.VMEM((heads, dim, 2 * dim), BF16),
            pltpu.VMEM((heads, dim, 2 * dim), BF16),
            pltpu.VMEM((heads, dim, 2 * dim), BF16),
            pltpu.VMEM((heads, dim, dim), F32),
            pltpu.SemaphoreType.DMA((3,)),
            pltpu.SemaphoreType.DMA((3,)),
            pltpu.SemaphoreType.DMA((3,)),
            pltpu.SemaphoreType.DMA((heads,)),
            pltpu.SemaphoreType.DMA((heads,)),
            pltpu.SemaphoreType.DMA((blks, heads)),
            pltpu.SemaphoreType.DMA((heads,)),
        ],
        compiler_params=pltpu.CompilerParams(
            collective_id=0, has_side_effects=True, vmem_limit_bytes=52 << 20),
    )(query_raw, key_raw, value_raw, conv_weight, beta_rate.T, out_gain.reshape(1, dim))


def solution(mesh):
    placed = (
        P(("groups", "seq", "blk"), "hd"),
        P(("groups", "seq", "blk"), "hd"),
        P(("groups", "seq", "blk"), "hd"),
        P(("groups", "seq", "blk"), "hd"),
        P(None, None, "hd"),
        P(),
    )
    return jax.shard_map(
        on_device,
        mesh=mesh,
        in_specs=placed,
        out_specs=P(("groups", "seq", "blk"), "hd"),
        check_vma=False,
    )
```

```python
import functools

import jax
import jax.numpy as jnp
from jax import lax
from jax.experimental import pallas as pl
from jax.experimental.pallas import tpu as pltpu
from jax.sharding import PartitionSpec as P

F32 = jnp.float32
BF16 = jnp.bfloat16
CHUNK = 128
RIM = 16
LEAD = 8
PAIR = 2
SMALL = 8
MESH = pl.DeviceIdType.MESH


def mm(a, b):
    return jnp.dot(a.astype(BF16), b.astype(BF16), preferred_element_type=F32)


def mm_nt(a, b):
    return lax.dot_general(a, b, (((1,), (1,)), ((), ())), preferred_element_type=F32)


def split(x):
    high = x.astype(BF16)
    return high, (x - high.astype(F32)).astype(BF16)


def mm3(a, b):
    a_high, a_low = split(a)
    b_high, b_low = split(b)
    return mm(a_high, b_high) + mm(a_high, b_low) + mm(a_low, b_high)


def layer_kernel(seqs, blks, taps, q_hbm, k_hbm, v_hbm, w_ref, beta_ref, gain_ref, o_ref,
                 raw, rim, pad, keys, wu_ref, state_ref, a_ref, b_ref, lead_ref, known_ref,
                 came, goes, before, onward, row_a, row_b, load_sem, rim_send, rim_recv,
                 join_send, join_recv, send_sem, recv_sem):
    rows = q_hbm.shape[0]
    heads, dim = b_ref.shape[0], b_ref.shape[-1]
    chunks = rows // CHUNK
    pairs = heads // PAIR
    total = seqs * blks
    z, x = lax.axis_index("seq"), lax.axis_index("blk")
    end = blks - 1
    here = z * blks + x
    lag = z + end
    sends_row = x < end
    sends_state = (x == end) & (z < seqs - 1)
    below = (z + 1) % seqs
    after = (here + 1) % total
    ahead = (here + total - 1) % total
    after_id = {"seq": after // blks, "blk": after % blks}
    ahead_id = {"seq": ahead // blks, "blk": ahead % blks}
    has_ahead = here > 0
    has_after = here < total - 1
    sources = (q_hbm, k_hbm, v_hbm)

    def load(which):
        return pltpu.make_async_copy(sources[which], raw.at[which], load_sem.at[which])

    def rim_move(which):
        return pltpu.make_async_remote_copy(
            src_ref=sources[which].at[pl.ds(rows - RIM, RIM)], dst_ref=rim.at[which],
            send_sem=rim_send.at[which], recv_sem=rim_recv.at[which],
            device_id=after_id, device_id_type=MESH)

    def join(head):
        return pltpu.make_async_remote_copy(
            src_ref=onward.at[head], dst_ref=before.at[head],
            send_sem=join_send.at[head], recv_sem=join_recv.at[head],
            device_id={"seq": z, "blk": (x + 1) % blks}, device_id_type=MESH)

    def move(head, target):
        return pltpu.make_async_remote_copy(
            src_ref=goes.at[head], dst_ref=came.at[head],
            send_sem=send_sem.at[target, head], recv_sem=recv_sem.at[head],
            device_id={"seq": below, "blk": target}, device_id_type=MESH)

    barrier = pltpu.get_barrier_semaphore()

    @pl.when(has_ahead)
    def _():
        pl.semaphore_signal(barrier, inc=1, device_id=ahead_id, device_id_type=MESH)

    @pl.when(has_after)
    def _():
        pl.semaphore_signal(barrier, inc=1, device_id=after_id, device_id_type=MESH)

    for which in (1, 2, 0):
        load(which).start()

    @pl.when(here == 0)
    def _():
        rim[...] = jnp.zeros_like(rim)

    @pl.when(z == 0)
    def _():
        came[...] = jnp.zeros_like(came)

    extra_up = (x > 0) & (z > 0)

    @pl.when(extra_up)
    def _():
        pl.semaphore_signal(barrier, inc=1, device_id={"seq": (z + seqs - 1) % seqs, "blk": end},
                            device_id_type=MESH)

    @pl.when(sends_state)
    def _():
        for target in range(1, blks):
            pl.semaphore_signal(barrier, inc=1, device_id={"seq": below, "blk": target},
                                device_id_type=MESH)

    pl.semaphore_wait(
        barrier,
        has_ahead.astype(jnp.int32) + has_after.astype(jnp.int32)
        + extra_up.astype(jnp.int32) + end * sends_state.astype(jnp.int32))

    @pl.when(has_after)
    def _():
        for which in (1, 2, 0):
            rim_move(which).start()

    def arrive(which):
        load(which).wait()

        @pl.when(has_ahead)
        def _():
            rim_move(which).wait_recv()

    arrive(1)
    arrive(2)

    row = lax.broadcasted_iota(jnp.int32, (CHUNK, CHUNK), 0)
    col = lax.broadcasted_iota(jnp.int32, (CHUNK, CHUNK), 1)
    head_row = lax.broadcasted_iota(jnp.int32, (heads, CHUNK), 0)
    eye = jnp.where(row == col, 1.0, 0.0)

    @pl.when(x == 0)
    def _():
        for head in range(heads):
            before[head] = jnp.concatenate((eye, jnp.zeros_like(eye)), axis=1).astype(BF16)

    def lanes_of(head):
        return pl.ds(pl.multiple_of(head * dim, dim), dim)

    def conv(which, head, slot):
        lanes = lanes_of(head)
        pad[slot, 0:LEAD] = rim[which, RIM - LEAD:RIM, lanes].astype(F32)
        pad[slot, LEAD:] = raw[which, :, lanes].astype(F32)
        summed = jnp.zeros((rows, dim), F32)
        for tap in range(taps):
            summed = summed + w_ref[which, tap:tap + 1, lanes] * pad[
                slot, pl.ds(LEAD - taps + 1 + tap, rows)]
        half = 0.5 * summed
        return half + half * jnp.tanh(half)

    def maps_of(pair):
        ks, vs, rates, flat = [], [], [], []
        for lane in range(PAIR):
            head = pair * PAIR + lane
            k = conv(1, head, lane * 2)
            k = (k * lax.rsqrt(jnp.sum(k * k, axis=-1, keepdims=True) + 1e-06)).astype(BF16)
            keys[:, lanes_of(head)] = k
            v = conv(2, head, lane * 2 + 1).astype(BF16)
            for c in range(chunks):
                part = slice(c * CHUNK, (c + 1) * CHUNK)
                ks.append(k[part])
                vs.append(v[part])
                flat.append(jnp.sum(jnp.where(head_row == head, beta_ref[:, part], 0.0), axis=0, keepdims=True))
                rates.append(jnp.sum(jnp.where(row == col, flat[-1], 0.0), axis=1, keepdims=True))
        lower = [jnp.where(col < row, r * mm_nt(k, k), 0.0) for r, k in zip(rates, ks)]
        near = row // SMALL == col // SMALL
        power = [jnp.where(near, x, 0.0) for x in lower]
        rest = [-x for x in power]
        power = [mm(x, x) for x in power]
        size = 4
        while size < SMALL:
            joint = [mm(jnp.concatenate((x, y), axis=0), y) for x, y in zip(rest, power)]
            rest = [x + y + z[:CHUNK] for x, y, z in zip(rest, power, joint)]
            power = [z[CHUNK:] for z in joint]
            size *= 2
        rest = [x + y + mm(x, y) for x, y in zip(rest, power)]
        size = SMALL
        while size < CHUNK:
            cuts = range(0, CHUNK, size)

            def odd(x):
                return jnp.concatenate([x[n:n + size] for n in cuts[1::2]], axis=0)

            def joined(evens, odds):
                rows_of = []
                for n, start in enumerate(cuts[0::2]):
                    rows_of.append(evens[start:start + size])
                    rows_of.append(odds[n * size:(n + 1) * size])
                return jnp.concatenate(rows_of, axis=0)

            band = odd(row // size) == odd(col // size) + 1
            blank = jnp.zeros((CHUNK, CHUNK), F32)
            off = [jnp.where(band, odd(x), 0.0) for x in lower]
            mid = [x + mm(x, y) for x, y in zip(off, rest)]
            rest = [
                joined(x, odd(x) - y - mm(odd(x), joined(blank, y))) for x, y in zip(rest, mid)
            ]
            size *= 2
        kv = [jnp.concatenate((k, v), axis=1) for k, v in zip(ks, vs)]
        wu = [r * x.astype(F32) + mm(t * f, x) for r, x, t, f in zip(rates, kv, rest, flat)]
        made = []
        for k, solved in zip(ks, wu):
            turned = k.astype(F32).T.astype(BF16)
            made.append(mm(jnp.concatenate((turned, turned), axis=1),
                           jnp.concatenate(split(solved), axis=0)))
        states = [jnp.concatenate((eye, jnp.zeros((dim, dim), F32)), axis=1)] * PAIR
        for c in range(chunks):
            part = slice(c * CHUNK, (c + 1) * CHUNK)
            for lane in range(PAIR):
                head = pair * PAIR + lane
                x = made[lane * chunks + c]
                wu_ref[head, part] = wu[lane * chunks + c]
                state_ref[head, part] = states[lane]
                step = x[:, :dim] if c else None
                written = jnp.concatenate((jnp.zeros((dim, dim), F32), x[:, dim:]), axis=1)
                if c:
                    states[lane] = states[lane] - mm(step, states[lane]) + written
                else:
                    states[lane] = jnp.concatenate((eye - x[:, :dim], x[:, dim:]), axis=1)
        for lane in range(PAIR):
            a_ref[pair * PAIR + lane] = jnp.concatenate(split(states[lane][:, :dim]), axis=1)
            b_ref[pair * PAIR + lane] = states[lane][:, dim:]

    def compose(pair):
        for lane in range(PAIR):
            head = pair * PAIR + lane

            @pl.when(x > 0)
            def _():
                join(head).wait_recv()

            prior = before[head]
            both = mm(a_ref[head], jnp.concatenate((prior, prior), axis=0))
            made_map, made_add = both[:, :dim], both[:, dim:] + b_ref[head]

            @pl.when(sends_row)
            def _():
                onward[head] = jnp.concatenate((made_map, made_add), axis=1).astype(BF16)
                join(head).start()

            @pl.when(sends_state)
            def _():
                row_a[head] = jnp.concatenate(split(made_map), axis=1)
                row_b[head] = made_add

    def pass_on(pair):
        for lane in range(PAIR):
            head = pair * PAIR + lane

            @pl.when(z > 0)
            def _():
                move(head, 0).wait_recv()

            @pl.when(sends_state)
            def _():
                state = came[head]
                goes[head] = (
                    row_b[head] + mm(row_a[head], jnp.concatenate((state, state), axis=0))
                ).astype(BF16)
                for target in range(blks - 1, -1, -1):
                    move(head, target).start()

    def reads_of(pair):
        for lane in range(PAIR):
            head = pair * PAIR + lane
            q = conv(0, head, lane).astype(BF16)
            for c in range(chunks):
                part = slice(c * CHUNK, (c + 1) * CHUNK)
                scores = jnp.where(col <= row, mm_nt(q[part], keys[part, lanes_of(head)]), 0.0)
                near = mm3(scores, wu_ref[head, part])
                y = mm3(q[part].astype(F32) - near[:, :dim], state_ref[head, part])
                lead_ref[head, part] = y[:, :dim]
                known_ref[head, part] = y[:, dim:] + near[:, dim:]

    def finish(pair):
        for lane in range(PAIR):
            head = pair * PAIR + lane
            prior = before[head]
            state = (mm(prior[:, :dim], came[head]) + prior[:, dim:].astype(F32)).astype(BF16)
            out = known_ref[head] + mm(
                jnp.concatenate(split(lead_ref[head]), axis=1),
                jnp.concatenate((state, state), axis=0))
            mean_sq = jnp.mean(out * out, axis=-1, keepdims=True)
            out = out * lax.rsqrt(mean_sq + 1e-05) * gain_ref[...]
            o_ref[:, lanes_of(head)] = out.astype(o_ref.dtype)

    def first_part(i, carry):
        maps_of(i)

        @pl.when((i >= x) & (i < x + pairs))
        def _():
            compose(i - x)

        @pl.when(i >= lag)
        def _():
            pass_on(i - lag)
        return carry

    def second_part(i, carry):
        reads_of(i - pairs)

        @pl.when((i >= x) & (i < x + pairs))
        def _():
            compose(i - x)

        @pl.when((i >= lag) & (i < lag + pairs))
        def _():
            pass_on(i - lag)

        @pl.when(lag <= pairs)
        def _():
            finish(i - pairs)

        @pl.when((lag > pairs) & (i >= lag))
        def _():
            finish(i - lag)
        return carry

    def third_part(i, carry):
        @pl.when((i >= x) & (i < x + pairs))
        def _():
            compose(i - x)

        @pl.when(i >= lag)
        def _():
            pass_on(i - lag)
            finish(i - lag)
        return carry

    lax.fori_loop(0, pairs, first_part, 0)
    arrive(0)
    lax.fori_loop(pairs, 2 * pairs, second_part, 0)
    lax.fori_loop(2 * pairs, lag + pairs, third_part, 0)

    @pl.when(has_after)
    def _():
        for which in range(3):
            rim_move(which).wait_send()

    @pl.when(sends_row)
    def _():
        for head in range(heads):
            join(head).wait_send()

    @pl.when(sends_state)
    def _():
        for head in range(heads):
            for target in range(blks):
                move(head, target).wait_send()


def on_device(query_raw, key_raw, value_raw, beta_rate, conv_weight, out_gain):
    rows, width = query_raw.shape
    heads = beta_rate.shape[1]
    dim = width // heads
    taps = conv_weight.shape[1]
    seqs, blks = lax.axis_size("seq"), lax.axis_size("blk")
    far = pl.BlockSpec(memory_space=pltpu.HBM)
    vmem = pl.BlockSpec(memory_space=pltpu.VMEM)
    return pl.pallas_call(
        functools.partial(layer_kernel, seqs, blks, taps),
        name="layer",
        out_shape=jax.ShapeDtypeStruct((rows, width), BF16),
        in_specs=[far, far, far, vmem, vmem, vmem],
        out_specs=vmem,
        scratch_shapes=[
            pltpu.VMEM((3, rows, width), BF16),
            pltpu.VMEM((3, RIM, width), BF16),
            pltpu.VMEM((2 * PAIR, rows + LEAD, dim), F32),
            pltpu.VMEM((rows, width), BF16),
            pltpu.VMEM((heads, rows, 2 * dim), F32),
            pltpu.VMEM((heads, rows, 2 * dim), F32),
            pltpu.VMEM((heads, dim, 2 * dim), BF16),
            pltpu.VMEM((heads, dim, dim), F32),
            pltpu.VMEM((heads, rows, dim), F32),
            pltpu.VMEM((heads, rows, dim), F32),
            pltpu.VMEM((heads, dim, dim), BF16),
            pltpu.VMEM((heads, dim, dim), BF16),
            pltpu.VMEM((heads, dim, 2 * dim), BF16),
            pltpu.VMEM((heads, dim, 2 * dim), BF16),
            pltpu.VMEM((heads, dim, 2 * dim), BF16),
            pltpu.VMEM((heads, dim, dim), F32),
            pltpu.SemaphoreType.DMA((3,)),
            pltpu.SemaphoreType.DMA((3,)),
            pltpu.SemaphoreType.DMA((3,)),
            pltpu.SemaphoreType.DMA((heads,)),
            pltpu.SemaphoreType.DMA((heads,)),
            pltpu.SemaphoreType.DMA((blks, heads)),
            pltpu.SemaphoreType.DMA((heads,)),
        ],
        compiler_params=pltpu.CompilerParams(
            collective_id=0, has_side_effects=True, vmem_limit_bytes=52 << 20),
    )(query_raw, key_raw, value_raw, conv_weight, beta_rate.T, out_gain.reshape(1, dim))


def solution(mesh):
    placed = (
        P(("groups", "seq", "blk"), "hd"),
        P(("groups", "seq", "blk"), "hd"),
        P(("groups", "seq", "blk"), "hd"),
        P(("groups", "seq", "blk"), "hd"),
        P(None, None, "hd"),
        P(),
    )
    return jax.shard_map(
        on_device,
        mesh=mesh,
        in_specs=placed,
        out_specs=P(("groups", "seq", "blk"), "hd"),
        check_vma=False,
    )
```

```python
import functools

import jax
import jax.numpy as jnp
from jax import lax
from jax.experimental import pallas as pl
from jax.experimental.pallas import tpu as pltpu
from jax.sharding import PartitionSpec as P

F32 = jnp.float32
BF16 = jnp.bfloat16
CHUNK = 128
RIM = 16
LEAD = 8
PAIR = 2
SMALL = 16
MESH = pl.DeviceIdType.MESH


def mm(a, b):
    return jnp.dot(a.astype(BF16), b.astype(BF16), preferred_element_type=F32)


def mm_nt(a, b):
    return lax.dot_general(a, b, (((1,), (1,)), ((), ())), preferred_element_type=F32)


def split(x):
    high = x.astype(BF16)
    return high, (x - high.astype(F32)).astype(BF16)


def mm3(a, b):
    a_high, a_low = split(a)
    b_high, b_low = split(b)
    return mm(a_high, b_high) + mm(a_high, b_low) + mm(a_low, b_high)


def layer_kernel(seqs, blks, taps, q_hbm, k_hbm, v_hbm, w_ref, beta_ref, gain_ref, o_ref,
                 raw, rim, pad, keys, wu_ref, state_ref, a_ref, b_ref, lead_ref, known_ref,
                 came, goes, before, onward, row_a, row_b, load_sem, rim_send, rim_recv,
                 join_send, join_recv, send_sem, recv_sem):
    rows = q_hbm.shape[0]
    heads, dim = b_ref.shape[0], b_ref.shape[-1]
    chunks = rows // CHUNK
    pairs = heads // PAIR
    total = seqs * blks
    z, x = lax.axis_index("seq"), lax.axis_index("blk")
    end = blks - 1
    here = z * blks + x
    lag = z + end
    sends_row = x < end
    sends_state = (x == end) & (z < seqs - 1)
    below = (z + 1) % seqs
    after = (here + 1) % total
    ahead = (here + total - 1) % total
    after_id = {"seq": after // blks, "blk": after % blks}
    ahead_id = {"seq": ahead // blks, "blk": ahead % blks}
    has_ahead = here > 0
    has_after = here < total - 1
    sources = (q_hbm, k_hbm, v_hbm)

    def load(which):
        return pltpu.make_async_copy(sources[which], raw.at[which], load_sem.at[which])

    def rim_move(which):
        return pltpu.make_async_remote_copy(
            src_ref=sources[which].at[pl.ds(rows - RIM, RIM)], dst_ref=rim.at[which],
            send_sem=rim_send.at[which], recv_sem=rim_recv.at[which],
            device_id=after_id, device_id_type=MESH)

    def join(head):
        return pltpu.make_async_remote_copy(
            src_ref=onward.at[head], dst_ref=before.at[head],
            send_sem=join_send.at[head], recv_sem=join_recv.at[head],
            device_id={"seq": z, "blk": (x + 1) % blks}, device_id_type=MESH)

    def move(head, target):
        return pltpu.make_async_remote_copy(
            src_ref=goes.at[head], dst_ref=came.at[head],
            send_sem=send_sem.at[target, head], recv_sem=recv_sem.at[head],
            device_id={"seq": below, "blk": target}, device_id_type=MESH)

    barrier = pltpu.get_barrier_semaphore()

    @pl.when(has_ahead)
    def _():
        pl.semaphore_signal(barrier, inc=1, device_id=ahead_id, device_id_type=MESH)

    @pl.when(has_after)
    def _():
        pl.semaphore_signal(barrier, inc=1, device_id=after_id, device_id_type=MESH)

    for which in (1, 2, 0):
        load(which).start()

    @pl.when(here == 0)
    def _():
        rim[...] = jnp.zeros_like(rim)

    @pl.when(z == 0)
    def _():
        came[...] = jnp.zeros_like(came)

    extra_up = (x > 0) & (z > 0)

    @pl.when(extra_up)
    def _():
        pl.semaphore_signal(barrier, inc=1, device_id={"seq": (z + seqs - 1) % seqs, "blk": end},
                            device_id_type=MESH)

    @pl.when(sends_state)
    def _():
        for target in range(1, blks):
            pl.semaphore_signal(barrier, inc=1, device_id={"seq": below, "blk": target},
                                device_id_type=MESH)

    pl.semaphore_wait(
        barrier,
        has_ahead.astype(jnp.int32) + has_after.astype(jnp.int32)
        + extra_up.astype(jnp.int32) + end * sends_state.astype(jnp.int32))

    @pl.when(has_after)
    def _():
        for which in (1, 2, 0):
            rim_move(which).start()

    def arrive(which):
        load(which).wait()

        @pl.when(has_ahead)
        def _():
            rim_move(which).wait_recv()

    arrive(1)
    arrive(2)

    row = lax.broadcasted_iota(jnp.int32, (CHUNK, CHUNK), 0)
    col = lax.broadcasted_iota(jnp.int32, (CHUNK, CHUNK), 1)
    head_row = lax.broadcasted_iota(jnp.int32, (heads, CHUNK), 0)
    eye = jnp.where(row == col, 1.0, 0.0)

    @pl.when(x == 0)
    def _():
        for head in range(heads):
            before[head] = jnp.concatenate((eye, jnp.zeros_like(eye)), axis=1).astype(BF16)

    def lanes_of(head):
        return pl.ds(pl.multiple_of(head * dim, dim), dim)

    def conv(which, head, slot):
        lanes = lanes_of(head)
        pad[slot, 0:LEAD] = rim[which, RIM - LEAD:RIM, lanes].astype(F32)
        pad[slot, LEAD:] = raw[which, :, lanes].astype(F32)
        summed = jnp.zeros((rows, dim), F32)
        for tap in range(taps):
            summed = summed + w_ref[which, tap:tap + 1, lanes] * pad[
                slot, pl.ds(LEAD - taps + 1 + tap, rows)]
        half = 0.5 * summed
        return half + half * jnp.tanh(half)

    def maps_of(pair):
        ks, vs, rates, flat = [], [], [], []
        for lane in range(PAIR):
            head = pair * PAIR + lane
            k = conv(1, head, lane * 2)
            k = (k * lax.rsqrt(jnp.sum(k * k, axis=-1, keepdims=True) + 1e-06)).astype(BF16)
            keys[:, lanes_of(head)] = k
            v = conv(2, head, lane * 2 + 1).astype(BF16)
            for c in range(chunks):
                part = slice(c * CHUNK, (c + 1) * CHUNK)
                ks.append(k[part])
                vs.append(v[part])
                flat.append(jnp.sum(jnp.where(head_row == head, beta_ref[:, part], 0.0), axis=0, keepdims=True))
                rates.append(jnp.sum(jnp.where(row == col, flat[-1], 0.0), axis=1, keepdims=True))
        lower = [jnp.where(col < row, r * mm_nt(k, k), 0.0) for r, k in zip(rates, ks)]
        near = row // SMALL == col // SMALL
        power = [jnp.where(near, x, 0.0) for x in lower]
        rest = [-x for x in power]
        power = [mm(x, x) for x in power]
        size = 4
        while size < SMALL:
            joint = [mm(jnp.concatenate((x, y), axis=0), y) for x, y in zip(rest, power)]
            rest = [x + y + z[:CHUNK] for x, y, z in zip(rest, power, joint)]
            power = [z[CHUNK:] for z in joint]
            size *= 2
        rest = [x + y + mm(x, y) for x, y in zip(rest, power)]
        size = SMALL
        while size < CHUNK:
            band = (row // (2 * size) == col // (2 * size)) & (row // size != col // size)
            off = [jnp.where(band, x, 0.0) for x in lower]
            mid = [x + mm(x, y) for x, y in zip(off, rest)]
            rest = [x - y - mm(x, y) for x, y in zip(rest, mid)]
            size *= 2
        kv = [jnp.concatenate((k, v), axis=1) for k, v in zip(ks, vs)]
        wu = [r * x.astype(F32) + mm(t * f, x) for r, x, t, f in zip(rates, kv, rest, flat)]
        made = []
        for k, solved in zip(ks, wu):
            turned = k.astype(F32).T.astype(BF16)
            made.append(mm(jnp.concatenate((turned, turned), axis=1),
                           jnp.concatenate(split(solved), axis=0)))
        states = [jnp.concatenate((eye, jnp.zeros((dim, dim), F32)), axis=1)] * PAIR
        for c in range(chunks):
            part = slice(c * CHUNK, (c + 1) * CHUNK)
            for lane in range(PAIR):
                head = pair * PAIR + lane
                x = made[lane * chunks + c]
                wu_ref[head, part] = wu[lane * chunks + c]
                state_ref[head, part] = states[lane]
                step = x[:, :dim] if c else None
                written = jnp.concatenate((jnp.zeros((dim, dim), F32), x[:, dim:]), axis=1)
                if c:
                    states[lane] = states[lane] - mm(step, states[lane]) + written
                else:
                    states[lane] = jnp.concatenate((eye - x[:, :dim], x[:, dim:]), axis=1)
        for lane in range(PAIR):
            a_ref[pair * PAIR + lane] = jnp.concatenate(split(states[lane][:, :dim]), axis=1)
            b_ref[pair * PAIR + lane] = states[lane][:, dim:]

    def compose(pair):
        for lane in range(PAIR):
            head = pair * PAIR + lane

            @pl.when(x > 0)
            def _():
                join(head).wait_recv()

            prior = before[head]
            both = mm(a_ref[head], jnp.concatenate((prior, prior), axis=0))
            made_map, made_add = both[:, :dim], both[:, dim:] + b_ref[head]

            @pl.when(sends_row)
            def _():
                onward[head] = jnp.concatenate((made_map, made_add), axis=1).astype(BF16)
                join(head).start()

            @pl.when(sends_state)
            def _():
                row_a[head] = jnp.concatenate(split(made_map), axis=1)
                row_b[head] = made_add

    def pass_on(pair):
        for lane in range(PAIR):
            head = pair * PAIR + lane

            @pl.when(z > 0)
            def _():
                move(head, 0).wait_recv()

            @pl.when(sends_state)
            def _():
                state = came[head]
                goes[head] = (
                    row_b[head] + mm(row_a[head], jnp.concatenate((state, state), axis=0))
                ).astype(BF16)
                move(head, blks - 1).start()

        @pl.when(sends_state)
        def _():
            for lane in range(PAIR):
                for target in range(blks - 1):
                    move(pair * PAIR + lane, target).start()

    def reads_of(pair):
        for lane in range(PAIR):
            head = pair * PAIR + lane
            q = conv(0, head, lane).astype(BF16)
            for c in range(chunks):
                part = slice(c * CHUNK, (c + 1) * CHUNK)
                scores = jnp.where(col <= row, mm_nt(q[part], keys[part, lanes_of(head)]), 0.0)
                near = mm3(scores, wu_ref[head, part])
                y = mm3(q[part].astype(F32) - near[:, :dim], state_ref[head, part])
                lead_ref[head, part] = y[:, :dim]
                known_ref[head, part] = y[:, dim:] + near[:, dim:]

    def finish(pair):
        for lane in range(PAIR):
            head = pair * PAIR + lane
            prior = before[head]
            state = (mm(prior[:, :dim], came[head]) + prior[:, dim:].astype(F32)).astype(BF16)
            out = known_ref[head] + mm(
                jnp.concatenate(split(lead_ref[head]), axis=1),
                jnp.concatenate((state, state), axis=0))
            mean_sq = jnp.mean(out * out, axis=-1, keepdims=True)
            out = out * lax.rsqrt(mean_sq + 1e-05) * gain_ref[...]
            o_ref[:, lanes_of(head)] = out.astype(o_ref.dtype)

    def first_part(i, carry):
        maps_of(i)

        @pl.when((i >= x) & (i < x + pairs))
        def _():
            compose(i - x)

        @pl.when(i >= lag)
        def _():
            pass_on(i - lag)
        return carry

    def second_part(i, carry):
        reads_of(i - pairs)

        @pl.when((i >= x) & (i < x + pairs))
        def _():
            compose(i - x)

        @pl.when((i >= lag) & (i < lag + pairs))
        def _():
            pass_on(i - lag)

        @pl.when(lag <= pairs)
        def _():
            finish(i - pairs)

        @pl.when((lag > pairs) & (i >= lag))
        def _():
            finish(i - lag)
        return carry

    def third_part(i, carry):
        @pl.when((i >= x) & (i < x + pairs))
        def _():
            compose(i - x)

        @pl.when(i >= lag)
        def _():
            pass_on(i - lag)
            finish(i - lag)
        return carry

    lax.fori_loop(0, pairs, first_part, 0)
    arrive(0)
    lax.fori_loop(pairs, 2 * pairs, second_part, 0)
    lax.fori_loop(2 * pairs, lag + pairs, third_part, 0)

    @pl.when(has_after)
    def _():
        for which in range(3):
            rim_move(which).wait_send()

    @pl.when(sends_row)
    def _():
        for head in range(heads):
            join(head).wait_send()

    @pl.when(sends_state)
    def _():
        for head in range(heads):
            for target in range(blks):
                move(head, target).wait_send()


def on_device(query_raw, key_raw, value_raw, beta_rate, conv_weight, out_gain):
    rows, width = query_raw.shape
    heads = beta_rate.shape[1]
    dim = width // heads
    taps = conv_weight.shape[1]
    seqs, blks = lax.axis_size("seq"), lax.axis_size("blk")
    far = pl.BlockSpec(memory_space=pltpu.HBM)
    vmem = pl.BlockSpec(memory_space=pltpu.VMEM)
    return pl.pallas_call(
        functools.partial(layer_kernel, seqs, blks, taps),
        name="layer",
        out_shape=jax.ShapeDtypeStruct((rows, width), BF16),
        in_specs=[far, far, far, vmem, vmem, vmem],
        out_specs=vmem,
        scratch_shapes=[
            pltpu.VMEM((3, rows, width), BF16),
            pltpu.VMEM((3, RIM, width), BF16),
            pltpu.VMEM((2 * PAIR, rows + LEAD, dim), F32),
            pltpu.VMEM((rows, width), BF16),
            pltpu.VMEM((heads, rows, 2 * dim), F32),
            pltpu.VMEM((heads, rows, 2 * dim), F32),
            pltpu.VMEM((heads, dim, 2 * dim), BF16),
            pltpu.VMEM((heads, dim, dim), F32),
            pltpu.VMEM((heads, rows, dim), F32),
            pltpu.VMEM((heads, rows, dim), F32),
            pltpu.VMEM((heads, dim, dim), BF16),
            pltpu.VMEM((heads, dim, dim), BF16),
            pltpu.VMEM((heads, dim, 2 * dim), BF16),
            pltpu.VMEM((heads, dim, 2 * dim), BF16),
            pltpu.VMEM((heads, dim, 2 * dim), BF16),
            pltpu.VMEM((heads, dim, dim), F32),
            pltpu.SemaphoreType.DMA((3,)),
            pltpu.SemaphoreType.DMA((3,)),
            pltpu.SemaphoreType.DMA((3,)),
            pltpu.SemaphoreType.DMA((heads,)),
            pltpu.SemaphoreType.DMA((heads,)),
            pltpu.SemaphoreType.DMA((blks, heads)),
            pltpu.SemaphoreType.DMA((heads,)),
        ],
        compiler_params=pltpu.CompilerParams(
            collective_id=0, has_side_effects=True, vmem_limit_bytes=52 << 20),
    )(query_raw, key_raw, value_raw, conv_weight, beta_rate.T, out_gain.reshape(1, dim))


def solution(mesh):
    placed = (
        P(("groups", "seq", "blk"), "hd"),
        P(("groups", "seq", "blk"), "hd"),
        P(("groups", "seq", "blk"), "hd"),
        P(("groups", "seq", "blk"), "hd"),
        P(None, None, "hd"),
        P(),
    )
    return jax.shard_map(
        on_device,
        mesh=mesh,
        in_specs=placed,
        out_specs=P(("groups", "seq", "blk"), "hd"),
        check_vma=False,
    )
```
